32 devices in a mesh: seq: 2 (over x), row: 16 (over z, y, core).
Axes of the slice: x: 2, y: 2, z: 4, core: 2. Of those that a mesh axis runs over, the one named last changes fastest.
Arguments:
- qm: float32 [2, 16, 7, 256, 256], P('seq', 'row'), parts along dimension 0, may hold values from 0.005 to 0.05
- qm1: float32 [2, 16, 7, 256, 256], P('seq', 'row'), parts along dimension 0, may hold values from 0.005 to 0.05
- qb: float32 [2, 16, 7, 256, 256], P('seq', 'row'), parts along dimension 0, may hold values from 0.05 to 2
- codes: int32 [2, 16, 256], P('seq', 'row'), parts along dimension 0, may hold values from 0 to 3
- energy_index: int32 [2, 16, 256, 256], P('seq', 'row'), parts along dimension 0, may hold values from 0 to 63
- turner: float32 [64], replicated, may hold values from -1 to 1.5
Outputs:
- qb_new: float32 [2, 16, 256, 256], P('seq', 'row'), parts along dimension 0
- qm1_new: float32 [2, 16, 256, 256], P('seq', 'row'), parts along dimension 0
- qm_new: float32 [2, 16, 256, 256], P('seq', 'row'), parts along dimension 0
The draws below stay inside these ranges and needn't reach their ends.
There are 2 independent parts, one for each index of `seq`. The reference program is written for one: setup_inputs(seed, part) draws one part's arguments, and reference() takes and returns one part's arrays. A program takes and returns all parts, laid end to end along the dimension named above; an argument that names none is the same for every part. Nothing has to cross between parts.
All inputs are finite; a program needn't handle non-finite values.
Results may differ from the reference program's by a relative error of at most 0.0003.
Values sent between devices are 32-bit elements; how exact they have to be, the bound alone decides.
A program may use at most 64 MiB of HBM per device.

```python
import math
import jax
import jax.numpy as jnp
import numpy as np
from jax import lax

B = 256
DIST = 8
CYCLES = 1
TABLE = 64
DM = 7
BLOCK_ROWS = 16


def plant(entries, own_key, smallest, top_value):
    index_at = [jax.random.randint(jax.random.fold_in(own_key, axis), (), 0, length) for axis, length in enumerate(entries.shape)]
    main_axis = entries.shape.index(max(entries.shape))
    beside = index_at[:main_axis] + [(index_at[main_axis] + 1) % entries.shape[main_axis]] + index_at[main_axis + 1:]
    return entries.at[tuple(index_at)].set(smallest).at[tuple(beside)].set(top_value)


def levels(key, extent, cuts, smallest, largest):
    factor_of, own = 1.0, jax.random.fold_in(key, 6)
    for axis_at, blocks in cuts:
        steps = jnp.exp(jax.random.uniform(jax.random.fold_in(own, axis_at), (blocks,), jnp.float32, smallest / len(cuts), largest / len(cuts)))
        factor_of = factor_of * jnp.repeat(steps, extent[axis_at] // blocks).reshape([-1 if axis == axis_at else 1 for axis in range(len(extent))])
    return factor_of


def setup_inputs(seed: int = 0, part: int = 0) -> dict:
    key_of = jax.random.split(jax.random.key(seed), 7)
    part_splits = jax.random.split(jax.random.fold_in(key_of[6], part), 7)
    qm = jnp.clip(jnp.exp(math.log(0.05) - 2.3025851 * jax.random.uniform(part_splits[0], (CYCLES, BLOCK_ROWS, DM, B, B), jnp.float32) ** levels(part_splits[0], (CYCLES, BLOCK_ROWS, DM, B, B), ((1, 16),), -0.2, 0.2)), 0.005, 0.05)
    qm1 = jnp.clip(jnp.exp(math.log(0.05) - 2.3025851 * jax.random.uniform(part_splits[1], (CYCLES, BLOCK_ROWS, DM, B, B), jnp.float32) ** levels(part_splits[1], (CYCLES, BLOCK_ROWS, DM, B, B), ((1, 16),), -0.2, 0.2)), 0.005, 0.05)
    qb = jnp.clip(jnp.exp(math.log(2.0) - 3.6888794 * jax.random.uniform(part_splits[2], (CYCLES, BLOCK_ROWS, DM, B, B), jnp.float32) ** levels(part_splits[2], (CYCLES, BLOCK_ROWS, DM, B, B), ((1, 16),), -0.2, 0.2)), 0.05, 2.0)
    codes = plant(jax.random.randint(part_splits[3], (CYCLES, BLOCK_ROWS, B), 0, 4), jax.random.fold_in(part_splits[3], 1), 0, 3).astype(jnp.int32)
    energy_index = plant(jax.random.randint(part_splits[4], (CYCLES, BLOCK_ROWS, B, B), 0, TABLE), jax.random.fold_in(part_splits[4], 1), 0, TABLE - 1).astype(jnp.int32)
    turner = jnp.clip(jax.random.uniform(key_of[5], (TABLE,), jnp.float32, -1.0, 1.5), -1.0, 1.5)
    return {"qm": qm, "qm1": qm1, "qb": qb, "codes": codes, "energy_index": energy_index, "turner": turner}


PAIRS = np.array([[0, 0, 0, 1], [0, 0, 1, 0], [0, 1, 0, 1], [1, 0, 1, 0]], dtype=np.float32)
HI = lax.Precision.HIGHEST


def unpaired(shift):
    offsets = jnp.arange(B, dtype=jnp.int32)
    diffs = (shift * B + offsets[None, :] - offsets[:, None]).astype(jnp.float32)
    values = 0.01 * jnp.exp(-diffs / (DIST * B))
    if shift == 0:
        values = jnp.where(diffs >= 0, values, jnp.float32(0.0))
    return values


def decay(level):
    offsets = jnp.arange(B, dtype=jnp.int32)
    diffs = ((DIST - level) * B + offsets[None, :] - offsets[:, None]).astype(jnp.float32)
    values = jnp.exp(-diffs / (DIST * B))
    if level == DIST:
        values = jnp.where(diffs >= 0, values, jnp.float32(0.0))
    return values


def pairing(first, second):
    table = jnp.asarray(PAIRS, dtype=jnp.float32)
    digits = jnp.arange(4, dtype=jnp.int32)
    left = (first[:, None] == digits[None, :]).astype(jnp.float32)
    right = (second[:, None] == digits[None, :]).astype(jnp.float32)
    return jnp.dot(jnp.dot(left, table, precision=HI), right.T, precision=HI)


def reference(qm, qm1, qb, codes, energy_index, turner):
    total = CYCLES * BLOCK_ROWS
    qm_flat = qm.reshape(total, DIST - 1, B, B)
    qm1_flat = qm1.reshape(total, DIST - 1, B, B)
    qb_flat = qb.reshape(total, DIST - 1, B, B)
    code_flat = codes.reshape(total, B)
    index_flat = energy_index.reshape(total, B, B)

    def one(block):
        live = block + DIST < total
        summed = jnp.zeros((B, B), jnp.float32)
        tails = jnp.zeros((B, B), jnp.float32)
        for shift in range(1, DIST):
            later = jnp.minimum(block + shift, total - 1)
            right = qm1_flat[later, DIST - shift - 1]
            summed = summed + jnp.dot(qm_flat[block, shift - 1], right, precision=HI)
            tails = tails + jnp.dot(unpaired(shift), right, precision=HI)
        closing = jnp.minimum(block + DIST, total - 1)
        allowed = pairing(code_flat[block], code_flat[closing])
        weight = jnp.exp(-jnp.take(turner, index_flat[block]))
        pair_new = allowed * weight * (1.0 + 0.8 * summed)
        branch = jnp.dot(pair_new, decay(DIST), precision=HI)
        for level in range(1, DIST):
            branch = branch + jnp.dot(qb_flat[block, level - 1], decay(level), precision=HI)
        branch = branch * (1.0 / (DIST * B))
        multi = summed + tails + jnp.dot(unpaired(0), branch, precision=HI)
        zero = jnp.float32(0.0)
        return jnp.where(live, pair_new, zero), jnp.where(live, branch, zero), jnp.where(live, multi, zero)

    pair_all, branch_all, multi_all = lax.map(one, jnp.arange(total, dtype=jnp.int32))
    shape = (CYCLES, BLOCK_ROWS, B, B)
    return pair_all.reshape(shape), branch_all.reshape(shape), multi_all.reshape(shape)
```

```python
import functools

import jax
import jax.numpy as jnp
from jax import lax
from jax.experimental import pallas as pl
from jax.experimental.pallas import tpu as pltpu
from jax.sharding import PartitionSpec as P

F32 = jnp.float32
BF16 = jnp.bfloat16

PLAN = {
    1: (4, (3, 4, 5, 6, 7)),
    3: (6, (1, 2, 3, 4, 5, 6, 7)),
    4: (8, (4, 5, 6)),
    5: (9, (3, 4, 5, 6, 7)),
    6: (14, (3, 6, 7)),
    7: (10, (1, 2, 3, 5, 6)),
}


def split(x):
    high = x.astype(BF16)
    return high, (x - high.astype(F32)).astype(BF16)


def mm(a, b):
    return jnp.dot(a, b, preferred_element_type=F32)


def dot3(a, b):
    ah, al = a
    bh, bl = b
    return mm(ah, bh) + (mm(ah, bl) + mm(al, bh))


def any_of(x, values):
    hit = x == values[0]
    for value in values[1:]:
        hit = jnp.logical_or(hit, x == value)
    return hit


def kernel(
    plan, width, qm, qm1, qb, eidx, codes, turner, pair_out, branch_out, multi_out,
    q_own, r_own, q_far, r_far, qb_in, e_in, code_in, acc, acc_far, partial_in, weight, row_sum,
    tri_h, tri_l, up_h, up_l,
    own_sem, q_send, q_recv, r_send, r_recv, rf_recv, load_sem, code_sem, part_sem,
):
    dm, block = qm.shape[0], qm.shape[1]
    dist = dm + 1
    live_rows = width - dist
    beta = 1.0 / (dist * block)
    me = lax.axis_index("row")
    live = me < live_rows

    def remote(src, dst, send, recv, device):
        return pltpu.make_async_remote_copy(
            src_ref=src, dst_ref=dst, send_sem=send, recv_sem=recv,
            device_id={"row": device}, device_id_type=pl.DeviceIdType.MESH,
        )

    def moved_rows(m):
        return [row for row, (_, shifts) in plan.items() if m in shifts]

    def own(m):
        rows = moved_rows(m)
        return jnp.logical_and(live, jnp.logical_not(any_of(me, rows))) if rows else live

    def direct(m):
        row = me - m
        ok = jnp.logical_and(row >= 0, row < live_rows)
        rows = moved_rows(m)
        return jnp.logical_and(ok, jnp.logical_not(any_of(row, rows))) if rows else ok

    def code_send():
        return remote(codes, code_in, code_sem.at[0], code_sem.at[1], me - dist)

    def q_copy(m, device):
        return remote(qm.at[m - 1], q_far.at[m - 1], q_send.at[m - 1], q_recv.at[m - 1], device)

    def r_copy(m, device):
        return remote(qm1.at[dm - m], r_own.at[m - 1], r_send.at[m - 1], r_recv.at[m - 1], device)

    def rf_copy(m, device):
        return remote(qm1.at[dm - m], r_far.at[m - 1], r_send.at[m - 1], rf_recv.at[m - 1], device)

    def part_copy(device):
        return remote(acc_far, partial_in, part_sem.at[0], part_sem.at[1], device)

    for m in range(1, dist):
        for row in moved_rows(m):
            device = plan[row][0]

            @pl.when(me == row)
            def _():
                q_copy(m, device).start()

            if row + m == device:

                @pl.when(me == device)
                def _():
                    pltpu.make_async_copy(qm1.at[dm - m], r_far.at[m - 1], rf_recv.at[m - 1]).start()

            else:

                @pl.when(me == row + m)
                def _():
                    rf_copy(m, device).start()

    for m in range(1, dist):

        @pl.when(direct(m))
        def _():
            r_copy(m, me - m).start()

    @pl.when(me >= dist)
    def _():
        code_send().start()

    loads = (
        pltpu.make_async_copy(qb, qb_in, load_sem.at[0]),
        pltpu.make_async_copy(eidx, e_in, load_sem.at[1]),
    )

    @pl.when(live)
    def _():
        for load in loads:
            load.start()

    for m in range(1, dist):

        @pl.when(own(m))
        def _():
            pltpu.make_async_copy(qm.at[m - 1], q_own.at[m - 1], own_sem.at[m - 1]).start()

    acc[...] = jnp.zeros_like(acc)
    acc_far[...] = jnp.zeros_like(acc_far)
    rows_i = lax.broadcasted_iota(jnp.int32, (block, block), 0)
    cols_i = lax.broadcasted_iota(jnp.int32, (block, block), 1)
    column = lax.broadcasted_iota(jnp.int32, (block, 1), 0)
    line = lax.broadcasted_iota(jnp.int32, (1, block), 1)

    @pl.when(live)
    def _():
        diff = (cols_i - rows_i).astype(F32)
        fall = jnp.where(diff >= 0, jnp.exp(diff * (-beta)), 0.0)
        tri_h[...], tri_l[...] = split(fall)
        up_h[...], up_l[...] = split(0.01 * fall)
        code_send().wait_recv()
        first = jnp.sum(jnp.where(rows_i == cols_i, codes[...].astype(F32), 0.0), axis=1, keepdims=True)
        both = first + code_in[...].astype(F32)
        allowed = jnp.where(jnp.logical_or(both == 3.0, both == 5.0), 1.0, 0.0)
        table = jnp.exp(-turner[...])
        entries = table.shape[1]
        table = jnp.concatenate([table, jnp.zeros((1, 128 - entries), F32)], axis=1)
        table = jnp.broadcast_to(table, (block, 128))
        loads[1].wait()
        for start in range(0, block, 128):
            part = pl.ds(start, 128)
            found = jnp.take_along_axis(table, e_in[:, part], axis=1, mode="promise_in_bounds")
            weight[:, part] = found * allowed[:, start : start + 128]
        loads[0].wait()
        total = jnp.zeros((block, block), F32)
        for e in range(1, dist):
            factor = jnp.exp((line - (dist - e) * block).astype(F32) * beta)
            total = total + qb_in[e - 1] * factor
        row_sum[...] = jnp.broadcast_to(jnp.sum(total, axis=1, keepdims=True), row_sum.shape)

    def product(m, q, r, total):
        right = r[m]
        total[0:block, :] += dot3(split(q[m]), split(right))
        fade = jnp.exp((-(m + 1) * block - column).astype(F32) * beta)
        total[block : block + 1, :] += jnp.sum(right * fade, axis=0, keepdims=True)

    def mask_of(cases):
        total = jnp.int32(0)
        for device, shifts in cases:
            total = total + jnp.where(me == device, sum(2 ** (m - 1) for m in shifts), 0)
        return total

    if plan:
        far_mask = mask_of(list(plan.values()))

        def far_step(m, rest):
            @pl.when(rest % 2 == 1)
            def _():
                q_copy(m + 1, 0).wait_recv()
                rf_copy(m + 1, 0).wait_recv()
                product(m, q_far, r_far, acc_far)

            return rest // 2

        lax.fori_loop(0, dm, far_step, far_mask)
        for row, (device, _) in plan.items():

            @pl.when(me == device)
            def _():
                part_copy(row).start()

    moved = mask_of([(row, shifts) for row, (_, shifts) in plan.items()])
    own_mask = jnp.where(live, 2**dm - 1 - moved, 0)

    def own_step(m, rest):
        @pl.when(rest % 2 == 1)
        def _():
            pltpu.make_async_copy(qm.at[m], q_own.at[m], own_sem.at[m]).wait()
            r_copy(m + 1, 0).wait_recv()
            product(m, q_own, r_own, acc)

        return rest // 2

    lax.fori_loop(0, dm, own_step, own_mask)

    if plan:

        @pl.when(any_of(me, list(plan)))
        def _():
            part_copy(0).wait_recv()
            acc[...] += partial_in[...]

    @pl.when(live)
    def _():
        summed = acc[0:block, :]
        pair = weight[...] * (1.0 + 0.8 * summed)
        pair_out[...] = pair
        outer = row_sum[:, 0:1] * jnp.exp(line.astype(F32) * (-beta))
        branch = (outer + dot3(split(pair), (tri_h[...], tri_l[...]))) * beta
        branch_out[...] = branch
        tails = 0.01 * jnp.exp(column.astype(F32) * beta) * acc[block : block + 1, :]
        multi_out[...] = summed + tails + dot3((up_h[...], up_l[...]), split(branch))

    @pl.when(jnp.logical_not(live))
    def _():
        for out in (pair_out, branch_out, multi_out):
            out[...] = jnp.zeros_like(out)

    for m in range(1, dist):
        rows = moved_rows(m)
        row = me - m

        @pl.when(jnp.logical_and(row >= 0, row < live_rows))
        def _():
            if rows and any(plan[r][0] == r + m for r in rows):
                stays = any_of(me, [r + m for r in rows if plan[r][0] == r + m])

                @pl.when(jnp.logical_not(stays))
                def _():
                    r_copy(m, 0).wait_send()

            else:
                r_copy(m, 0).wait_send()

        if rows:

            @pl.when(any_of(me, rows))
            def _():
                q_copy(m, 0).wait_send()

    @pl.when(me >= dist)
    def _():
        code_send().wait_send()

    if plan:

        @pl.when(any_of(me, [device for device, _ in plan.values()]))
        def _():
            part_copy(0).wait_send()


def solution(mesh):
    width = mesh.shape["row"]

    def per_device(qm, qm1, qb, codes, energy_index, turner):
        dm, block = qm.shape[2], qm.shape[3]
        dist = dm + 1
        plan = PLAN if width == 16 and dist == 8 else {}
        blocks = pltpu.VMEM((dm, block, block), F32)
        whole = pltpu.VMEM((block, block), F32)
        half = pltpu.VMEM((block, block), BF16)
        tall = pltpu.VMEM((block + 8, block), F32)
        dma = pltpu.SemaphoreType.DMA
        anywhere = pl.BlockSpec(memory_space=pl.ANY)
        local = pl.BlockSpec(memory_space=pltpu.VMEM)
        outs = pl.pallas_call(
            functools.partial(kernel, plan, width),
            out_shape=[jax.ShapeDtypeStruct((block, block), F32)] * 3,
            in_specs=[anywhere] * 4 + [local] * 2,
            out_specs=[local] * 3,
            scratch_shapes=[
                blocks, blocks, blocks, blocks, blocks,
                pltpu.VMEM((block, block), jnp.int32),
                pltpu.VMEM((1, block), jnp.int32),
                tall, tall, tall, whole,
                pltpu.VMEM((block, 128), F32),
                half, half, half, half,
                dma((dm,)), dma((dm,)), dma((dm,)), dma((dm,)), dma((dm,)), dma((dm,)),
                dma((2,)), dma((2,)), dma((2,)),
            ],
            compiler_params=pltpu.CompilerParams(has_side_effects=True),
        )(
            qm[0, 0], qm1[0, 0], qb[0, 0], energy_index[0, 0],
            codes[0], turner[None, :],
        )
        return tuple(out[None, None] for out in outs)

    return jax.shard_map(
        per_device,
        mesh=mesh,
        in_specs=(
            P("seq", "row", None, None, None),
            P("seq", "row", None, None, None),
            P("seq", "row", None, None, None),
            P("seq", "row", None),
            P("seq", "row", None, None),
            P(),
        ),
        out_specs=(
            P("seq", "row", None, None),
            P("seq", "row", None, None),
            P("seq", "row", None, None),
        ),
        check_vma=False,
    )
```

```python
import functools

import jax
import jax.numpy as jnp
from jax import lax
from jax.experimental import pallas as pl
from jax.experimental.pallas import tpu as pltpu
from jax.sharding import PartitionSpec as P

F32 = jnp.float32
BF16 = jnp.bfloat16

PLAN = {
    1: (5, (3, 4, 5, 6, 7)),
    3: (7, (1, 2, 3, 5, 6)),
    4: (9, (5, 7)),
    5: (8, (3, 4, 5, 6, 7)),
    6: (10, (2, 3, 6, 7)),
    7: (15, (1, 5, 6)),
}
CHUNKS = 4


def split(x):
    high = x.astype(BF16)
    return high, (x - high.astype(F32)).astype(BF16)


def mm(a, b):
    return jnp.dot(a, b, preferred_element_type=F32)


def dot3(a, b):
    ah, al = a
    bh, bl = b
    return mm(ah, bh) + (mm(ah, bl) + mm(al, bh))


def any_of(x, values):
    hit = x == values[0]
    for value in values[1:]:
        hit = jnp.logical_or(hit, x == value)
    return hit


def kernel(
    plan, width, qm, qm1, qb, eidx, codes, turner, pair_out, branch_out, multi_out,
    q_own, r_own, q_far, r_far, rf_h, rf_l, qb_in, e_in, code_in, acc, acc_far, partial_in, weight, row_sum,
    tri_h, tri_l, up_h, up_l,
    own_sem, q_send, q_recv, r_send, r_recv, rf_recv, load_sem, code_sem, part_sem,
):
    dm, block = qm.shape[0], qm.shape[1]
    dist = dm + 1
    live_rows = width - dist
    beta = 1.0 / (dist * block)
    me = lax.axis_index("row")
    live = me < live_rows

    def remote(src, dst, send, recv, device):
        return pltpu.make_async_remote_copy(
            src_ref=src, dst_ref=dst, send_sem=send, recv_sem=recv,
            device_id={"row": device}, device_id_type=pl.DeviceIdType.MESH,
        )

    def moved_rows(m):
        return [row for row, (_, shifts) in plan.items() if m in shifts]

    def own(m):
        rows = moved_rows(m)
        return jnp.logical_and(live, jnp.logical_not(any_of(me, rows))) if rows else live

    def direct(m):
        row = me - m
        ok = jnp.logical_and(row >= 0, row < live_rows)
        rows = moved_rows(m)
        return jnp.logical_and(ok, jnp.logical_not(any_of(row, rows))) if rows else ok

    def code_send():
        return remote(codes, code_in, code_sem.at[0], code_sem.at[1], me - dist)

    height = block // CHUNKS

    def rows_of(c):
        return pl.ds(c * height, height)

    def q_copy(m, c, device):
        at = (m - 1, rows_of(c))
        return remote(qm.at[at], q_far.at[at], q_send.at[m - 1, c], q_recv.at[m - 1, c], device)

    def r_copy(m, device):
        return remote(qm1.at[dm - m], r_own.at[m - 1], r_send.at[m - 1], r_recv.at[m - 1], device)

    def rf_copy(m, device):
        return remote(qm1.at[dm - m], r_far.at[m - 1], r_send.at[m - 1], rf_recv.at[m - 1], device)

    def part_copy(c, device):
        at = pl.ds(c * height, height + (8 if c == CHUNKS - 1 else 0))
        return remote(acc_far.at[at], partial_in.at[at], part_sem.at[0, c], part_sem.at[1, c], device)

    @pl.when(me >= dist)
    def _():
        code_send().start()

    for m in range(1, dist):
        for row in moved_rows(m):
            device = plan[row][0]

            if row + m == device:

                @pl.when(me == device)
                def _():
                    pltpu.make_async_copy(qm1.at[dm - m], r_far.at[m - 1], rf_recv.at[m - 1]).start()

            else:

                @pl.when(me == row + m)
                def _():
                    rf_copy(m, device).start()

    for row, (device, shifts) in plan.items():

        @pl.when(me == row)
        def _():
            for c in range(CHUNKS):
                for m in shifts:
                    q_copy(m, c, device).start()

    for m in range(1, dist):

        @pl.when(direct(m))
        def _():
            r_copy(m, me - m).start()

    loads = (
        pltpu.make_async_copy(qb, qb_in, load_sem.at[0]),
        pltpu.make_async_copy(eidx, e_in, load_sem.at[1]),
    )

    @pl.when(live)
    def _():
        for load in loads:
            load.start()

    for m in range(1, dist):

        @pl.when(own(m))
        def _():
            pltpu.make_async_copy(qm.at[m - 1], q_own.at[m - 1], own_sem.at[m - 1]).start()

    acc[...] = jnp.zeros_like(acc)
    acc_far[...] = jnp.zeros_like(acc_far)
    rows_i = lax.broadcasted_iota(jnp.int32, (block, block), 0)
    cols_i = lax.broadcasted_iota(jnp.int32, (block, block), 1)
    column = lax.broadcasted_iota(jnp.int32, (block, 1), 0)
    line = lax.broadcasted_iota(jnp.int32, (1, block), 1)

    @pl.when(live)
    def _():
        diff = (cols_i - rows_i).astype(F32)
        fall = jnp.where(diff >= 0, jnp.exp(diff * (-beta)), 0.0)
        tri_h[...], tri_l[...] = split(fall)
        up_h[...], up_l[...] = split(0.01 * fall)
        code_send().wait_recv()
        first = jnp.sum(jnp.where(rows_i == cols_i, codes[...].astype(F32), 0.0), axis=1, keepdims=True)
        both = first + code_in[...].astype(F32)
        allowed = jnp.where(jnp.logical_or(both == 3.0, both == 5.0), 1.0, 0.0)
        table = jnp.exp(-turner[...])
        entries = table.shape[1]
        table = jnp.concatenate([table, jnp.zeros((1, 128 - entries), F32)], axis=1)
        table = jnp.broadcast_to(table, (block, 128))
        loads[1].wait()
        for start in range(0, block, 128):
            part = pl.ds(start, 128)
            found = jnp.take_along_axis(table, e_in[:, part], axis=1, mode="promise_in_bounds")
            weight[:, part] = found * allowed[:, start : start + 128]
        loads[0].wait()
        total = jnp.zeros((block, block), F32)
        for e in range(1, dist):
            factor = jnp.exp((line - (dist - e) * block).astype(F32) * beta)
            total = total + qb_in[e - 1] * factor
        row_sum[...] = jnp.broadcast_to(jnp.sum(total, axis=1, keepdims=True), row_sum.shape)

    def column_sum(m, right, total):
        fade = jnp.exp((-(m + 1) * block - column).astype(F32) * beta)
        total[block : block + 1, :] += jnp.sum(right * fade, axis=0, keepdims=True)

    def mask_of(cases):
        total = jnp.int32(0)
        for device, shifts in cases:
            total = total + jnp.where(me == device, sum(2 ** (m - 1) for m in shifts), 0)
        return total

    if plan:
        far_mask = mask_of(list(plan.values()))
        for c in range(CHUNKS):
            at = rows_of(c)

            def far_step(m, rest):
                @pl.when(rest % 2 == 1)
                def _():
                    if c == 0:
                        rf_copy(m + 1, 0).wait_recv()
                        right = r_far[m]
                        rf_h[m], rf_l[m] = split(right)
                        column_sum(m, right, acc_far)
                    q_copy(m + 1, c, 0).wait_recv()
                    acc_far[at, :] += dot3(split(q_far[m, at, :]), (rf_h[m], rf_l[m]))

                return rest // 2

            lax.fori_loop(0, dm, far_step, far_mask)
            for row, (device, _) in plan.items():

                @pl.when(me == device)
                def _():
                    part_copy(c, row).start()

    moved = mask_of([(row, shifts) for row, (_, shifts) in plan.items()])
    own_mask = jnp.where(live, 2**dm - 1 - moved, 0)

    def own_step(m, rest):
        @pl.when(rest % 2 == 1)
        def _():
            pltpu.make_async_copy(qm.at[m], q_own.at[m], own_sem.at[m]).wait()
            r_copy(m + 1, 0).wait_recv()
            right = r_own[m]
            column_sum(m, right, acc)
            acc[0:block, :] += dot3(split(q_own[m]), split(right))

        return rest // 2

    lax.fori_loop(0, dm, own_step, own_mask)

    if plan:

        @pl.when(any_of(me, list(plan)))
        def _():
            for c in range(CHUNKS):
                part_copy(c, 0).wait_recv()
            acc[...] += partial_in[...]

    @pl.when(live)
    def _():
        summed = acc[0:block, :]
        pair = weight[...] * (1.0 + 0.8 * summed)
        pair_out[...] = pair
        outer = row_sum[:, 0:1] * jnp.exp(line.astype(F32) * (-beta))
        branch = (outer + dot3(split(pair), (tri_h[...], tri_l[...]))) * beta
        branch_out[...] = branch
        tails = 0.01 * jnp.exp(column.astype(F32) * beta) * acc[block : block + 1, :]
        multi_out[...] = summed + tails + dot3((up_h[...], up_l[...]), split(branch))

    for m in range(1, dist):
        rows = moved_rows(m)
        row = me - m

        @pl.when(jnp.logical_and(row >= 0, row < live_rows))
        def _():
            if rows and any(plan[r][0] == r + m for r in rows):
                stays = any_of(me, [r + m for r in rows if plan[r][0] == r + m])

                @pl.when(jnp.logical_not(stays))
                def _():
                    r_copy(m, 0).wait_send()

            else:
                r_copy(m, 0).wait_send()

        if rows:

            @pl.when(any_of(me, rows))
            def _():
                for c in range(CHUNKS):
                    q_copy(m, c, 0).wait_send()

    @pl.when(me >= dist)
    def _():
        code_send().wait_send()

    if plan:

        @pl.when(any_of(me, [device for device, _ in plan.values()]))
        def _():
            for c in range(CHUNKS):
                part_copy(c, 0).wait_send()


def solution(mesh):
    width = mesh.shape["row"]

    def per_device(qm, qm1, qb, codes, energy_index, turner):
        dm, block = qm.shape[2], qm.shape[3]
        dist = dm + 1
        plan = PLAN if width == 16 and dist == 8 else {}
        blocks = pltpu.VMEM((dm, block, block), F32)
        halves = pltpu.VMEM((dm, block, block), BF16)
        whole = pltpu.VMEM((block, block), F32)
        half = pltpu.VMEM((block, block), BF16)
        tall = pltpu.VMEM((block + 8, block), F32)
        dma = pltpu.SemaphoreType.DMA
        anywhere = pl.BlockSpec(memory_space=pl.ANY)
        local = pl.BlockSpec(memory_space=pltpu.VMEM)
        outs = pl.pallas_call(
            functools.partial(kernel, plan, width),
            out_shape=[jax.ShapeDtypeStruct((block, block), F32)] * 3,
            in_specs=[anywhere] * 4 + [local] * 2,
            out_specs=[local] * 3,
            scratch_shapes=[
                blocks, blocks, blocks, blocks, halves, halves, blocks,
                pltpu.VMEM((block, block), jnp.int32),
                pltpu.VMEM((1, block), jnp.int32),
                tall, tall, tall, whole,
                pltpu.VMEM((block, 128), F32),
                half, half, half, half,
                dma((dm,)), dma((dm, CHUNKS)), dma((dm, CHUNKS)), dma((dm,)), dma((dm,)), dma((dm,)),
                dma((2,)), dma((2,)), dma((2, CHUNKS)),
            ],
            compiler_params=pltpu.CompilerParams(has_side_effects=True),
        )(
            qm[0, 0], qm1[0, 0], qb[0, 0], energy_index[0, 0],
            codes[0], turner[None, :],
        )
        live = lax.axis_index("row") < width - dist
        return tuple(jnp.where(live, out, 0.0)[None, None] for out in outs)

    return jax.shard_map(
        per_device,
        mesh=mesh,
        in_specs=(
            P("seq", "row", None, None, None),
            P("seq", "row", None, None, None),
            P("seq", "row", None, None, None),
            P("seq", "row", None),
            P("seq", "row", None, None),
            P(),
        ),
        out_specs=(
            P("seq", "row", None, None),
            P("seq", "row", None, None),
            P("seq", "row", None, None),
        ),
        check_vma=False,
    )
```

```python
import functools

import jax
import jax.numpy as jnp
from jax import lax
from jax.experimental import pallas as pl
from jax.experimental.pallas import tpu as pltpu
from jax.sharding import PartitionSpec as P

F32 = jnp.float32
BF16 = jnp.bfloat16

PLAN = {
    1: (5, (3, 4, 5, 6, 7)),
    2: (7, (2, 3, 4, 5, 6, 7)),
    4: (9, (4, 5, 6, 7)),
    5: (8, (3, 4, 6, 7)),
    6: (11, (3, 6, 7)),
    7: (10, (1, 2, 3, 5, 6)),
}
CHUNKS = 4


def split(x):
    high = x.astype(BF16)
    return high, (x - high.astype(F32)).astype(BF16)


def mm(a, b):
    return jnp.dot(a, b, preferred_element_type=F32)


def dot3(a, b):
    ah, al = a
    bh, bl = b
    return mm(ah, bh) + (mm(ah, bl) + mm(al, bh))


def any_of(x, values):
    hit = x == values[0]
    for value in values[1:]:
        hit = jnp.logical_or(hit, x == value)
    return hit


def kernel(
    plan, width, qm, qm1, qb, eidx, codes, turner, acc, weight, row_sum,
    q_own, r_own, q_far, r_far, rf_h, rf_l, qb_in, e_in, code_in, acc_far, partial_in,
    own_sem, q_send, q_recv, r_send, r_recv, rf_recv, load_sem, code_sem, part_sem,
):
    dm, block = qm.shape[0], qm.shape[1]
    dist = dm + 1
    live_rows = width - dist
    beta = 1.0 / (dist * block)
    me = lax.axis_index("row")
    live = me < live_rows

    def remote(src, dst, send, recv, device):
        return pltpu.make_async_remote_copy(
            src_ref=src, dst_ref=dst, send_sem=send, recv_sem=recv,
            device_id={"row": device}, device_id_type=pl.DeviceIdType.MESH,
        )

    def moved_rows(m):
        return [row for row, (_, shifts) in plan.items() if m in shifts]

    def own(m):
        rows = moved_rows(m)
        return jnp.logical_and(live, jnp.logical_not(any_of(me, rows))) if rows else live

    def direct(m):
        row = me - m
        ok = jnp.logical_and(row >= 0, row < live_rows)
        rows = moved_rows(m)
        return jnp.logical_and(ok, jnp.logical_not(any_of(row, rows))) if rows else ok

    def code_send():
        return remote(codes, code_in, code_sem.at[0], code_sem.at[1], me - dist)

    height = block // CHUNKS

    def rows_of(c):
        return pl.ds(c * height, height)

    def q_copy(m, c, device):
        at = (m - 1, rows_of(c))
        return remote(qm.at[at], q_far.at[at], q_send.at[m - 1, c], q_recv.at[m - 1, c], device)

    def r_copy(m, device):
        return remote(qm1.at[dm - m], r_own.at[m - 1], r_send.at[m - 1], r_recv.at[m - 1], device)

    def rf_copy(m, device):
        return remote(qm1.at[dm - m], r_far.at[m - 1], r_send.at[m - 1], rf_recv.at[m - 1], device)

    def part_copy(c, device):
        at = pl.ds(c * height, height + (8 if c == CHUNKS - 1 else 0))
        return remote(acc_far.at[at], partial_in.at[at], part_sem.at[0, c], part_sem.at[1, c], device)

    @pl.when(me >= dist)
    def _():
        code_send().start()

    for m in range(dm, 0, -1):
        for row in moved_rows(m):
            device = plan[row][0]

            if row + m == device:

                @pl.when(me == device)
                def _():
                    pltpu.make_async_copy(qm1.at[dm - m], r_far.at[m - 1], rf_recv.at[m - 1]).start()

            else:

                @pl.when(me == row + m)
                def _():
                    rf_copy(m, device).start()

    for row, (device, shifts) in plan.items():

        @pl.when(me == row)
        def _():
            for c in range(CHUNKS):
                for m in reversed(shifts):
                    q_copy(m, c, device).start()

    for m in range(dm, 0, -1):

        @pl.when(direct(m))
        def _():
            r_copy(m, me - m).start()

    loads = (
        pltpu.make_async_copy(qb, qb_in, load_sem.at[0]),
        pltpu.make_async_copy(eidx, e_in, load_sem.at[1]),
    )

    @pl.when(live)
    def _():
        for load in loads:
            load.start()

    for m in range(1, dist):

        @pl.when(own(m))
        def _():
            pltpu.make_async_copy(qm.at[m - 1], q_own.at[m - 1], own_sem.at[m - 1]).start()

    acc[...] = jnp.zeros_like(acc)
    acc_far[...] = jnp.zeros_like(acc_far)
    rows_i = lax.broadcasted_iota(jnp.int32, (block, block), 0)
    cols_i = lax.broadcasted_iota(jnp.int32, (block, block), 1)
    column = lax.broadcasted_iota(jnp.int32, (block, 1), 0)
    line = lax.broadcasted_iota(jnp.int32, (1, block), 1)

    @pl.when(live)
    def _():
        code_send().wait_recv()
        first = jnp.sum(jnp.where(rows_i == cols_i, codes[...].astype(F32), 0.0), axis=1, keepdims=True)
        both = first + code_in[...].astype(F32)
        allowed = jnp.where(jnp.logical_or(both == 3.0, both == 5.0), 1.0, 0.0)
        table = jnp.exp(-turner[...])
        entries = table.shape[1]
        table = jnp.concatenate([table, jnp.zeros((1, 128 - entries), F32)], axis=1)
        table = jnp.broadcast_to(table, (block, 128))
        loads[1].wait()
        for start in range(0, block, 128):
            part = pl.ds(start, 128)
            found = jnp.take_along_axis(table, e_in[:, part], axis=1, mode="promise_in_bounds")
            weight[:, part] = found * allowed[:, start : start + 128]
        loads[0].wait()
        total = jnp.zeros((block, block), F32)
        for e in range(1, dist):
            factor = jnp.exp((line - (dist - e) * block).astype(F32) * beta)
            total = total + qb_in[e - 1] * factor
        row_sum[...] = jnp.broadcast_to(jnp.sum(total, axis=1, keepdims=True), row_sum.shape)

    def column_sum(m, right, total):
        fade = jnp.exp((-(m + 1) * block - column).astype(F32) * beta)
        total[block : block + 1, :] += jnp.sum(right * fade, axis=0, keepdims=True)

    def mask_of(cases):
        total = jnp.int32(0)
        for device, shifts in cases:
            total = total + jnp.where(me == device, sum(2 ** (dm - m) for m in shifts), 0)
        return total

    if plan:
        far_mask = mask_of(list(plan.values()))
        for c in range(CHUNKS):
            at = rows_of(c)

            def far_step(step, rest):
                m = dm - 1 - step

                @pl.when(rest % 2 == 1)
                def _():
                    if c == 0:
                        rf_copy(m + 1, 0).wait_recv()
                        right = r_far[m]
                        rf_h[m], rf_l[m] = split(right)
                        column_sum(m, right, acc_far)
                    q_copy(m + 1, c, 0).wait_recv()
                    acc_far[at, :] += dot3(split(q_far[m, at, :]), (rf_h[m], rf_l[m]))

                return rest // 2

            lax.fori_loop(0, dm, far_step, far_mask)
            for row, (device, _) in plan.items():

                @pl.when(me == device)
                def _():
                    part_copy(c, row).start()

    moved = mask_of([(row, shifts) for row, (_, shifts) in plan.items()])
    own_mask = jnp.where(live, 2**dm - 1 - moved, 0)

    def own_step(step, rest):
        m = dm - 1 - step

        @pl.when(rest % 2 == 1)
        def _():
            pltpu.make_async_copy(qm.at[m], q_own.at[m], own_sem.at[m]).wait()
            r_copy(m + 1, 0).wait_recv()
            right = r_own[m]
            column_sum(m, right, acc)
            acc[0:block, :] += dot3(split(q_own[m]), split(right))

        return rest // 2

    lax.fori_loop(0, dm, own_step, own_mask)

    if plan:

        @pl.when(any_of(me, list(plan)))
        def _():
            for c in range(CHUNKS):
                part_copy(c, 0).wait_recv()
            acc[...] += partial_in[...]

    for m in range(1, dist):
        rows = moved_rows(m)
        row = me - m

        @pl.when(jnp.logical_and(row >= 0, row < live_rows))
        def _():
            if rows and any(plan[r][0] == r + m for r in rows):
                stays = any_of(me, [r + m for r in rows if plan[r][0] == r + m])

                @pl.when(jnp.logical_not(stays))
                def _():
                    r_copy(m, 0).wait_send()

            else:
                r_copy(m, 0).wait_send()

        if rows:

            @pl.when(any_of(me, rows))
            def _():
                for c in range(CHUNKS):
                    q_copy(m, c, 0).wait_send()

    @pl.when(me >= dist)
    def _():
        code_send().wait_send()

    if plan:

        @pl.when(any_of(me, [device for device, _ in plan.values()]))
        def _():
            for c in range(CHUNKS):
                part_copy(c, 0).wait_send()


def finish(live_rows, dist, acc, weight, row_sum, pair_out, branch_out, multi_out):
    block = weight.shape[0]
    beta = 1.0 / (dist * block)
    live = lax.axis_index("row") < live_rows

    @pl.when(live)
    def _():
        column = lax.broadcasted_iota(jnp.int32, (block, 1), 0).astype(F32)
        line = lax.broadcasted_iota(jnp.int32, (1, block), 1).astype(F32)
        rows_i = lax.broadcasted_iota(jnp.int32, (block, block), 0)
        cols_i = lax.broadcasted_iota(jnp.int32, (block, block), 1)
        upper = jnp.where(cols_i >= rows_i, 1.0, 0.0).astype(BF16)
        summed = acc[0:block, :]
        pair = weight[...] * (1.0 + 0.8 * summed)
        pair_out[...] = pair
        high, low = split(pair * jnp.exp(line * beta))
        inner = mm(high, upper) + mm(low, upper)
        branch = (row_sum[:, 0:1] + inner) * (beta * jnp.exp(line * (-beta)))
        branch_out[...] = branch
        high, low = split(branch * jnp.exp(column * (-beta)))
        tails = acc[block : block + 1, :] + mm(upper, high) + mm(upper, low)
        multi_out[...] = summed + 0.01 * jnp.exp(column * beta) * tails

    @pl.when(jnp.logical_not(live))
    def _():
        for out in (pair_out, branch_out, multi_out):
            out[...] = jnp.zeros_like(out)


def solution(mesh):
    width = mesh.shape["row"]

    def per_device(qm, qm1, qb, codes, energy_index, turner):
        dm, block = qm.shape[2], qm.shape[3]
        dist = dm + 1
        plan = PLAN if width == 16 and dist == 8 else {}
        blocks = pltpu.VMEM((dm, block, block), F32)
        halves = pltpu.VMEM((dm, block, block), BF16)
        square = jax.ShapeDtypeStruct((block, block), F32)
        tall = pltpu.VMEM((block + 8, block), F32)
        dma = pltpu.SemaphoreType.DMA
        anywhere = pl.BlockSpec(memory_space=pltpu.HBM)
        local = pl.BlockSpec(memory_space=pltpu.VMEM)
        middle = pl.pallas_call(
            functools.partial(kernel, plan, width),
            out_shape=[
                pltpu.VMEM((block + 8, block), F32),
                pltpu.VMEM((block, block), F32),
                pltpu.VMEM((block, 128), F32),
            ],
            in_specs=[anywhere] * 4 + [local] * 2,
            out_specs=[local] * 3,
            scratch_shapes=[
                blocks, blocks, blocks, blocks, halves, halves, blocks,
                pltpu.VMEM((block, block), jnp.int32),
                pltpu.VMEM((1, block), jnp.int32),
                tall, tall,
                dma((dm,)), dma((dm, CHUNKS)), dma((dm, CHUNKS)), dma((dm,)), dma((dm,)), dma((dm,)),
                dma((2,)), dma((2,)), dma((2, CHUNKS)),
            ],
            compiler_params=pltpu.CompilerParams(has_side_effects=True),
        )(
            qm[0, 0], qm1[0, 0], qb[0, 0], energy_index[0, 0],
            codes[0], turner[None, :],
        )
        outs = pl.pallas_call(
            functools.partial(finish, width - dist, dist),
            out_shape=[square] * 3,
            in_specs=[local] * 3,
            out_specs=[local] * 3,
            compiler_params=pltpu.CompilerParams(vmem_limit_bytes=16 * 2**20),
        )(*middle)
        return tuple(out[None, None] for out in outs)

    return jax.shard_map(
        per_device,
        mesh=mesh,
        in_specs=(
            P("seq", "row", None, None, None),
            P("seq", "row", None, None, None),
            P("seq", "row", None, None, None),
            P("seq", "row", None),
            P("seq", "row", None, None),
            P(),
        ),
        out_specs=(
            P("seq", "row", None, None),
            P("seq", "row", None, None),
            P("seq", "row", None, None),
        ),
        check_vma=False,
    )
```

```python
import functools

import jax
import jax.numpy as jnp
from jax import lax
from jax.experimental import pallas as pl
from jax.experimental.pallas import tpu as pltpu
from jax.sharding import PartitionSpec as P

F32 = jnp.float32
BF16 = jnp.bfloat16

PLAN = {
    1: (5, (3, 4, 5, 6, 7)),
    2: (6, (2, 4, 5, 6, 7)),
    4: (8, (4, 5, 6)),
    5: (9, (3, 5, 6, 7)),
    6: (10, (2, 3, 7)),
    7: (15, (1, 2, 5, 6)),
}
CHUNKS = 4


def split(x):
    high = x.astype(BF16)
    return high, (x - high.astype(F32)).astype(BF16)


def mm(a, b):
    return jnp.dot(a, b, preferred_element_type=F32)


def dot3(a, b):
    ah, al = a
    bh, bl = b
    return mm(ah, bh) + (mm(ah, bl) + mm(al, bh))


def any_of(x, values):
    hit = x == values[0]
    for value in values[1:]:
        hit = jnp.logical_or(hit, x == value)
    return hit


def kernel(
    plan, width, qm, qm1, qb, eidx, codes, turner, acc, weight, row_sum,
    q_own, r_own, q_far, r_far, rf_h, rf_l, qb_in, e_in, code_in, acc_far, partial_in,
    own_sem, q_send, q_recv, r_send, r_recv, rf_recv, load_sem, code_sem, part_sem,
):
    dm, block = qm.shape[0], qm.shape[1]
    dist = dm + 1
    live_rows = width - dist
    beta = 1.0 / (dist * block)
    me = lax.axis_index("row")
    live = me < live_rows

    def remote(src, dst, send, recv, device):
        return pltpu.make_async_remote_copy(
            src_ref=src, dst_ref=dst, send_sem=send, recv_sem=recv,
            device_id={"row": device}, device_id_type=pl.DeviceIdType.MESH,
        )

    def moved_rows(m):
        return [row for row, (_, shifts) in plan.items() if m in shifts]

    def own(m):
        rows = moved_rows(m)
        return jnp.logical_and(live, jnp.logical_not(any_of(me, rows))) if rows else live

    def direct(m):
        row = me - m
        ok = jnp.logical_and(row >= 0, row < live_rows)
        rows = moved_rows(m)
        return jnp.logical_and(ok, jnp.logical_not(any_of(row, rows))) if rows else ok

    def code_send():
        return remote(codes, code_in, code_sem.at[0], code_sem.at[1], me - dist)

    height = block // CHUNKS

    def rows_of(c):
        return pl.ds(c * height, height)

    def q_copy(m, c, device):
        at = (m - 1, rows_of(c))
        return remote(qm.at[at], q_far.at[at], q_send.at[m - 1, c], q_recv.at[m - 1, c], device)

    def r_copy(m, device):
        return remote(qm1.at[dm - m], r_own.at[m - 1], r_send.at[m - 1], r_recv.at[m - 1], device)

    def rf_copy(m, device):
        return remote(qm1.at[dm - m], r_far.at[m - 1], r_send.at[m - 1], rf_recv.at[m - 1], device)

    def part_copy(c, device):
        at = pl.ds(c * height, height + (8 if c == CHUNKS - 1 else 0))
        return remote(acc_far.at[at], partial_in.at[at], part_sem.at[0, c], part_sem.at[1, c], device)

    @pl.when(me >= dist)
    def _():
        code_send().start()

    for m in range(dm, 0, -1):
        for row in moved_rows(m):
            device = plan[row][0]

            if row + m == device:

                @pl.when(me == device)
                def _():
                    pltpu.make_async_copy(qm1.at[dm - m], r_far.at[m - 1], rf_recv.at[m - 1]).start()

            else:

                @pl.when(me == row + m)
                def _():
                    rf_copy(m, device).start()

    for row, (device, shifts) in plan.items():

        @pl.when(me == row)
        def _():
            for c in range(CHUNKS):
                for m in reversed(shifts):
                    q_copy(m, c, device).start()

    for m in range(dm, 0, -1):

        @pl.when(direct(m))
        def _():
            r_copy(m, me - m).start()

    loads = (
        pltpu.make_async_copy(qb, qb_in, load_sem.at[0]),
        pltpu.make_async_copy(eidx, e_in, load_sem.at[1]),
    )

    @pl.when(live)
    def _():
        for load in loads:
            load.start()

    for m in range(1, dist):

        @pl.when(own(m))
        def _():
            pltpu.make_async_copy(qm.at[m - 1], q_own.at[m - 1], own_sem.at[m - 1]).start()

    acc[...] = jnp.zeros_like(acc)
    acc_far[...] = jnp.zeros_like(acc_far)
    rows_i = lax.broadcasted_iota(jnp.int32, (block, block), 0)
    cols_i = lax.broadcasted_iota(jnp.int32, (block, block), 1)
    column = lax.broadcasted_iota(jnp.int32, (block, 1), 0)
    line = lax.broadcasted_iota(jnp.int32, (1, block), 1)

    @pl.when(live)
    def _():
        code_send().wait_recv()
        first = jnp.sum(jnp.where(rows_i == cols_i, codes[...].astype(F32), 0.0), axis=1, keepdims=True)
        both = first + code_in[...].astype(F32)
        allowed = jnp.where(jnp.logical_or(both == 3.0, both == 5.0), 1.0, 0.0)
        table = jnp.exp(-turner[...])
        entries = table.shape[1]
        table = jnp.concatenate([table, jnp.zeros((1, 128 - entries), F32)], axis=1)
        table = jnp.broadcast_to(table, (block, 128))
        loads[1].wait()
        for start in range(0, block, 128):
            part = pl.ds(start, 128)
            found = jnp.take_along_axis(table, e_in[:, part], axis=1, mode="promise_in_bounds")
            weight[:, part] = found * allowed[:, start : start + 128]
        loads[0].wait()
        total = jnp.zeros((block, block), F32)
        for e in range(1, dist):
            factor = jnp.exp((line - (dist - e) * block).astype(F32) * beta)
            total = total + qb_in[e - 1] * factor
        row_sum[...] = jnp.broadcast_to(jnp.sum(total, axis=1, keepdims=True), row_sum.shape)

    def column_sum(m, right, total):
        fade = jnp.exp((-(m + 1) * block - column).astype(F32) * beta)
        total[block : block + 1, :] += jnp.sum(right * fade, axis=0, keepdims=True)

    def mask_of(cases):
        total = jnp.int32(0)
        for device, shifts in cases:
            total = total + jnp.where(me == device, sum(2 ** (dm - m) for m in shifts), 0)
        return total

    if plan:
        far_mask = mask_of(list(plan.values()))
        for c in range(CHUNKS):
            at = rows_of(c)

            def far_step(step, rest):
                m = dm - 1 - step

                @pl.when(rest % 2 == 1)
                def _():
                    if c == 0:
                        rf_copy(m + 1, 0).wait_recv()
                        right = r_far[m]
                        rf_h[m], rf_l[m] = split(right)
                        column_sum(m, right, acc_far)
                    q_copy(m + 1, c, 0).wait_recv()
                    acc_far[at, :] += dot3(split(q_far[m, at, :]), (rf_h[m], rf_l[m]))

                return rest // 2

            lax.fori_loop(0, dm, far_step, far_mask)
            for row, (device, _) in plan.items():

                @pl.when(me == device)
                def _():
                    part_copy(c, row).start()

    moved = mask_of([(row, shifts) for row, (_, shifts) in plan.items()])
    own_mask = jnp.where(live, 2**dm - 1 - moved, 0)

    def own_step(step, rest):
        m = dm - 1 - step

        @pl.when(rest % 2 == 1)
        def _():
            pltpu.make_async_copy(qm.at[m], q_own.at[m], own_sem.at[m]).wait()
            r_copy(m + 1, 0).wait_recv()
            right = r_own[m]
            column_sum(m, right, acc)
            acc[0:block, :] += dot3(split(q_own[m]), split(right))

        return rest // 2

    lax.fori_loop(0, dm, own_step, own_mask)

    if plan:

        @pl.when(any_of(me, list(plan)))
        def _():
            for c in range(CHUNKS):
                part_copy(c, 0).wait_recv()
            acc[...] += partial_in[...]

    for m in range(1, dist):
        rows = moved_rows(m)
        row = me - m

        @pl.when(jnp.logical_and(row >= 0, row < live_rows))
        def _():
            if rows and any(plan[r][0] == r + m for r in rows):
                stays = any_of(me, [r + m for r in rows if plan[r][0] == r + m])

                @pl.when(jnp.logical_not(stays))
                def _():
                    r_copy(m, 0).wait_send()

            else:
                r_copy(m, 0).wait_send()

        if rows:

            @pl.when(any_of(me, rows))
            def _():
                for c in range(CHUNKS):
                    q_copy(m, c, 0).wait_send()

    @pl.when(me >= dist)
    def _():
        code_send().wait_send()

    if plan:

        @pl.when(any_of(me, [device for device, _ in plan.values()]))
        def _():
            for c in range(CHUNKS):
                part_copy(c, 0).wait_send()


def finish(live_rows, dist, acc, weight, row_sum, pair_out, branch_out, multi_out):
    block = weight.shape[0]
    beta = 1.0 / (dist * block)
    live = lax.axis_index("row") < live_rows

    @pl.when(live)
    def _():
        column = lax.broadcasted_iota(jnp.int32, (block, 1), 0).astype(F32)
        line = lax.broadcasted_iota(jnp.int32, (1, block), 1).astype(F32)
        rows_i = lax.broadcasted_iota(jnp.int32, (block, block), 0)
        cols_i = lax.broadcasted_iota(jnp.int32, (block, block), 1)
        upper = jnp.where(cols_i >= rows_i, 1.0, 0.0).astype(BF16)
        summed = acc[0:block, :]
        pair = weight[...] * (1.0 + 0.8 * summed)
        pair_out[...] = pair
        high, low = split(pair * jnp.exp(line * beta))
        inner = mm(high, upper) + mm(low, upper)
        branch = (row_sum[:, 0:1] + inner) * (beta * jnp.exp(line * (-beta)))
        branch_out[...] = branch
        high, low = split(branch * jnp.exp(column * (-beta)))
        tails = acc[block : block + 1, :] + mm(upper, high) + mm(upper, low)
        multi_out[...] = summed + 0.01 * jnp.exp(column * beta) * tails

    @pl.when(jnp.logical_not(live))
    def _():
        for out in (pair_out, branch_out, multi_out):
            out[...] = jnp.zeros_like(out)


def solution(mesh):
    width = mesh.shape["row"]

    def per_device(qm, qm1, qb, codes, energy_index, turner):
        dm, block = qm.shape[2], qm.shape[3]
        dist = dm + 1
        plan = PLAN if width == 16 and dist == 8 else {}
        blocks = pltpu.VMEM((dm, block, block), F32)
        halves = pltpu.VMEM((dm, block, block), BF16)
        square = jax.ShapeDtypeStruct((block, block), F32)
        tall = pltpu.VMEM((block + 8, block), F32)
        dma = pltpu.SemaphoreType.DMA
        anywhere = pl.BlockSpec(memory_space=pltpu.HBM)
        local = pl.BlockSpec(memory_space=pltpu.VMEM)
        middle = pl.pallas_call(
            functools.partial(kernel, plan, width),
            out_shape=[
                pltpu.VMEM((block + 8, block), F32),
                pltpu.VMEM((block, block), F32),
                pltpu.VMEM((block, 128), F32),
            ],
            in_specs=[anywhere] * 4 + [local] * 2,
            out_specs=[local] * 3,
            scratch_shapes=[
                blocks, blocks, blocks, blocks, halves, halves, blocks,
                pltpu.VMEM((block, block), jnp.int32),
                pltpu.VMEM((1, block), jnp.int32),
                tall, tall,
                dma((dm,)), dma((dm, CHUNKS)), dma((dm, CHUNKS)), dma((dm,)), dma((dm,)), dma((dm,)),
                dma((2,)), dma((2,)), dma((2, CHUNKS)),
            ],
            compiler_params=pltpu.CompilerParams(has_side_effects=True),
        )(
            qm[0, 0], qm1[0, 0], qb[0, 0], energy_index[0, 0],
            codes[0], turner[None, :],
        )
        outs = pl.pallas_call(
            functools.partial(finish, width - dist, dist),
            out_shape=[square] * 3,
            in_specs=[local] * 3,
            out_specs=[local] * 3,
            compiler_params=pltpu.CompilerParams(vmem_limit_bytes=16 * 2**20),
        )(*middle)
        return tuple(out[None, None] for out in outs)

    return jax.shard_map(
        per_device,
        mesh=mesh,
        in_specs=(
            P("seq", "row", None, None, None),
            P("seq", "row", None, None, None),
            P("seq", "row", None, None, None),
            P("seq", "row", None),
            P("seq", "row", None, None),
            P(),
        ),
        out_specs=(
            P("seq", "row", None, None),
            P("seq", "row", None, None),
            P("seq", "row", None, None),
        ),
        check_vma=False,
    )
```

```python
import functools

import jax
import jax.numpy as jnp
from jax import lax
from jax.experimental import pallas as pl
from jax.experimental.pallas import tpu as pltpu
from jax.sharding import PartitionSpec as P

F32 = jnp.float32
BF16 = jnp.bfloat16

PLAN = {
    1: (5, (3, 4, 5, 6, 7)),
    2: (6, (2, 4, 5, 6, 7)),
    4: (8, (4, 5, 6)),
    5: (9, (3, 5, 6, 7)),
    6: (10, (2, 3, 7)),
    7: (15, (1, 2, 5, 6)),
}
CHUNKS = 2


def split(x):
    high = x.astype(BF16)
    return high, (x - high.astype(F32)).astype(BF16)


def mm(a, b):
    return jnp.dot(a, b, preferred_element_type=F32)


def dot3(a, b):
    ah, al = a
    bh, bl = b
    return mm(ah, bh) + (mm(ah, bl) + mm(al, bh))


def any_of(x, values):
    hit = x == values[0]
    for value in values[1:]:
        hit = jnp.logical_or(hit, x == value)
    return hit


def kernel(
    plan, width, qm, qm1, qb, eidx, codes, turner, acc, weight, row_sum,
    q_own, r_own, q_far, r_far, rf_h, rf_l, qb_in, e_in, code_in, acc_far, partial_in,
    own_sem, q_send, q_recv, r_send, r_recv, rf_recv, load_sem, code_sem, part_sem,
):
    dm, block = qm.shape[0], qm.shape[1]
    dist = dm + 1
    live_rows = width - dist
    beta = 1.0 / (dist * block)
    me = lax.axis_index("row")
    live = me < live_rows

    def remote(src, dst, send, recv, device):
        return pltpu.make_async_remote_copy(
            src_ref=src, dst_ref=dst, send_sem=send, recv_sem=recv,
            device_id={"row": device}, device_id_type=pl.DeviceIdType.MESH,
        )

    def moved_rows(m):
        return [row for row, (_, shifts) in plan.items() if m in shifts]

    def own(m):
        rows = moved_rows(m)
        return jnp.logical_and(live, jnp.logical_not(any_of(me, rows))) if rows else live

    def direct(m):
        row = me - m
        ok = jnp.logical_and(row >= 0, row < live_rows)
        rows = moved_rows(m)
        return jnp.logical_and(ok, jnp.logical_not(any_of(row, rows))) if rows else ok

    def code_send():
        return remote(codes, code_in, code_sem.at[0], code_sem.at[1], me - dist)

    height = block // CHUNKS

    def rows_of(c):
        return pl.ds(c * height, height)

    def q_copy(m, c, device):
        at = (m - 1, rows_of(c))
        return remote(qm.at[at], q_far.at[at], q_send.at[m - 1, c], q_recv.at[m - 1, c], device)

    def r_copy(m, device):
        return remote(qm1.at[dm - m], r_own.at[m - 1], r_send.at[m - 1], r_recv.at[m - 1], device)

    def rf_copy(m, device):
        return remote(qm1.at[dm - m], r_far.at[m - 1], r_send.at[m - 1], rf_recv.at[m - 1], device)

    def part_copy(c, device):
        at = pl.ds(c * height, height + (8 if c == CHUNKS - 1 else 0))
        return remote(acc_far.at[at], partial_in.at[at], part_sem.at[0, c], part_sem.at[1, c], device)

    barrier = pltpu.get_barrier_semaphore()

    def greet(device):
        pl.semaphore_signal(
            barrier, inc=1, device_id={"row": device}, device_id_type=pl.DeviceIdType.MESH
        )

    extra = set()
    for row, (device, shifts) in plan.items():
        extra |= {(row, device), (device, row)} | {(row + m, device) for m in shifts}
    extra = sorted((s, d) for s, d in extra if s != d and not (d < live_rows and 1 <= s - d <= dist))

    @pl.when(live)
    def _():
        for m in range(1, dist + 1):
            greet(me + m)

    for source, device in extra:

        @pl.when(me == device)
        def _():
            greet(source)

    awaited = jnp.int32(0)
    for m in range(1, dist + 1):
        row = me - m
        awaited = awaited + jnp.where(jnp.logical_and(row >= 0, row < live_rows), 1, 0)
    for source, _ in extra:
        awaited = awaited + jnp.where(me == source, 1, 0)

    @pl.when(awaited > 0)
    def _():
        pl.semaphore_wait(barrier, awaited)

    @pl.when(me >= dist)
    def _():
        code_send().start()

    for m in range(dm, 0, -1):
        for row in moved_rows(m):
            device = plan[row][0]

            if row + m == device:

                @pl.when(me == device)
                def _():
                    pltpu.make_async_copy(qm1.at[dm - m], r_far.at[m - 1], rf_recv.at[m - 1]).start()

            else:

                @pl.when(me == row + m)
                def _():
                    rf_copy(m, device).start()

    for row, (device, shifts) in plan.items():

        @pl.when(me == row)
        def _():
            for c in range(CHUNKS):
                for m in reversed(shifts):
                    q_copy(m, c, device).start()

    for m in range(dm, 0, -1):

        @pl.when(direct(m))
        def _():
            r_copy(m, me - m).start()

    loads = (
        pltpu.make_async_copy(qb, qb_in, load_sem.at[0]),
        pltpu.make_async_copy(eidx, e_in, load_sem.at[1]),
    )

    @pl.when(live)
    def _():
        for load in loads:
            load.start()

    for m in range(1, dist):

        @pl.when(own(m))
        def _():
            pltpu.make_async_copy(qm.at[m - 1], q_own.at[m - 1], own_sem.at[m - 1]).start()

    acc[...] = jnp.zeros_like(acc)
    acc_far[...] = jnp.zeros_like(acc_far)
    rows_i = lax.broadcasted_iota(jnp.int32, (block, block), 0)
    cols_i = lax.broadcasted_iota(jnp.int32, (block, block), 1)
    column = lax.broadcasted_iota(jnp.int32, (block, 1), 0)
    line = lax.broadcasted_iota(jnp.int32, (1, block), 1)

    @pl.when(live)
    def _():
        code_send().wait_recv()
        first = jnp.sum(jnp.where(rows_i == cols_i, codes[...].astype(F32), 0.0), axis=1, keepdims=True)
        both = first + code_in[...].astype(F32)
        allowed = jnp.where(jnp.logical_or(both == 3.0, both == 5.0), 1.0, 0.0)
        table = jnp.exp(-turner[...])
        entries = table.shape[1]
        table = jnp.concatenate([table, jnp.zeros((1, 128 - entries), F32)], axis=1)
        table = jnp.broadcast_to(table, (block, 128))
        loads[1].wait()
        for start in range(0, block, 128):
            part = pl.ds(start, 128)
            found = jnp.take_along_axis(table, e_in[:, part], axis=1, mode="promise_in_bounds")
            weight[:, part] = found * allowed[:, start : start + 128]
        loads[0].wait()
        total = jnp.zeros((block, block), F32)
        for e in range(1, dist):
            factor = jnp.exp((line - (dist - e) * block).astype(F32) * beta)
            total = total + qb_in[e - 1] * factor
        row_sum[...] = jnp.broadcast_to(jnp.sum(total, axis=1, keepdims=True), row_sum.shape)

    def column_sum(m, right, total):
        fade = jnp.exp((-(m + 1) * block - column).astype(F32) * beta)
        total[block : block + 1, :] += jnp.sum(right * fade, axis=0, keepdims=True)

    def mask_of(cases):
        total = jnp.int32(0)
        for device, shifts in cases:
            total = total + jnp.where(me == device, sum(2 ** (dm - m) for m in shifts), 0)
        return total

    if plan:
        far_mask = mask_of(list(plan.values()))
        for c in range(CHUNKS):
            at = rows_of(c)

            def far_step(step, rest):
                m = dm - 1 - step

                @pl.when(rest % 2 == 1)
                def _():
                    if c == 0:
                        rf_copy(m + 1, 0).wait_recv()
                        right = r_far[m]
                        rf_h[m], rf_l[m] = split(right)
                        column_sum(m, right, acc_far)
                    q_copy(m + 1, c, 0).wait_recv()
                    acc_far[at, :] += dot3(split(q_far[m, at, :]), (rf_h[m], rf_l[m]))

                return rest // 2

            lax.fori_loop(0, dm, far_step, far_mask)
            for row, (device, _) in plan.items():

                @pl.when(me == device)
                def _():
                    part_copy(c, row).start()

    moved = mask_of([(row, shifts) for row, (_, shifts) in plan.items()])
    own_mask = jnp.where(live, 2**dm - 1 - moved, 0)

    def own_step(step, rest):
        m = dm - 1 - step

        @pl.when(rest % 2 == 1)
        def _():
            pltpu.make_async_copy(qm.at[m], q_own.at[m], own_sem.at[m]).wait()
            r_copy(m + 1, 0).wait_recv()
            right = r_own[m]
            column_sum(m, right, acc)
            acc[0:block, :] += dot3(split(q_own[m]), split(right))

        return rest // 2

    lax.fori_loop(0, dm, own_step, own_mask)

    if plan:

        @pl.when(any_of(me, list(plan)))
        def _():
            for c in range(CHUNKS):
                part_copy(c, 0).wait_recv()
            acc[...] += partial_in[...]

    for m in range(1, dist):
        rows = moved_rows(m)
        row = me - m

        @pl.when(jnp.logical_and(row >= 0, row < live_rows))
        def _():
            if rows and any(plan[r][0] == r + m for r in rows):
                stays = any_of(me, [r + m for r in rows if plan[r][0] == r + m])

                @pl.when(jnp.logical_not(stays))
                def _():
                    r_copy(m, 0).wait_send()

            else:
                r_copy(m, 0).wait_send()

        if rows:

            @pl.when(any_of(me, rows))
            def _():
                for c in range(CHUNKS):
                    q_copy(m, c, 0).wait_send()

    @pl.when(me >= dist)
    def _():
        code_send().wait_send()

    if plan:

        @pl.when(any_of(me, [device for device, _ in plan.values()]))
        def _():
            for c in range(CHUNKS):
                part_copy(c, 0).wait_send()


def finish(live_rows, dist, acc, weight, row_sum, pair_out, branch_out, multi_out):
    block = weight.shape[0]
    beta = 1.0 / (dist * block)
    live = lax.axis_index("row") < live_rows

    @pl.when(live)
    def _():
        column = lax.broadcasted_iota(jnp.int32, (block, 1), 0).astype(F32)
        line = lax.broadcasted_iota(jnp.int32, (1, block), 1).astype(F32)
        rows_i = lax.broadcasted_iota(jnp.int32, (block, block), 0)
        cols_i = lax.broadcasted_iota(jnp.int32, (block, block), 1)
        upper = jnp.where(cols_i >= rows_i, 1.0, 0.0).astype(BF16)
        summed = acc[0:block, :]
        pair = weight[...] * (1.0 + 0.8 * summed)
        pair_out[...] = pair
        high, low = split(pair * jnp.exp(line * beta))
        inner = mm(high, upper) + mm(low, upper)
        branch = (row_sum[:, 0:1] + inner) * (beta * jnp.exp(line * (-beta)))
        branch_out[...] = branch
        high, low = split(branch * jnp.exp(column * (-beta)))
        tails = acc[block : block + 1, :] + mm(upper, high) + mm(upper, low)
        multi_out[...] = summed + 0.01 * jnp.exp(column * beta) * tails

    @pl.when(jnp.logical_not(live))
    def _():
        for out in (pair_out, branch_out, multi_out):
            out[...] = jnp.zeros_like(out)


def solution(mesh):
    width = mesh.shape["row"]

    def per_device(qm, qm1, qb, codes, energy_index, turner):
        dm, block = qm.shape[2], qm.shape[3]
        dist = dm + 1
        plan = PLAN if width == 16 and dist == 8 else {}
        blocks = pltpu.VMEM((dm, block, block), F32)
        halves = pltpu.VMEM((dm, block, block), BF16)
        square = jax.ShapeDtypeStruct((block, block), F32)
        tall = pltpu.VMEM((block + 8, block), F32)
        dma = pltpu.SemaphoreType.DMA
        anywhere = pl.BlockSpec(memory_space=pltpu.HBM)
        local = pl.BlockSpec(memory_space=pltpu.VMEM)
        middle = pl.pallas_call(
            functools.partial(kernel, plan, width),
            out_shape=[
                pltpu.VMEM((block + 8, block), F32),
                pltpu.VMEM((block, block), F32),
                pltpu.VMEM((block, 128), F32),
            ],
            in_specs=[anywhere] * 4 + [local] * 2,
            out_specs=[local] * 3,
            scratch_shapes=[
                blocks, blocks, blocks, blocks, halves, halves, blocks,
                pltpu.VMEM((block, block), jnp.int32),
                pltpu.VMEM((1, block), jnp.int32),
                tall, tall,
                dma((dm,)), dma((dm, CHUNKS)), dma((dm, CHUNKS)), dma((dm,)), dma((dm,)), dma((dm,)),
                dma((2,)), dma((2,)), dma((2, CHUNKS)),
            ],
            compiler_params=pltpu.CompilerParams(has_side_effects=True, collective_id=0),
        )(
            qm[0, 0], qm1[0, 0], qb[0, 0], energy_index[0, 0],
            codes[0], turner[None, :],
        )
        outs = pl.pallas_call(
            functools.partial(finish, width - dist, dist),
            out_shape=[square] * 3,
            in_specs=[local] * 3,
            out_specs=[local] * 3,
            compiler_params=pltpu.CompilerParams(vmem_limit_bytes=16 * 2**20),
        )(*middle)
        return tuple(out[None, None] for out in outs)

    return jax.shard_map(
        per_device,
        mesh=mesh,
        in_specs=(
            P("seq", "row", None, None, None),
            P("seq", "row", None, None, None),
            P("seq", "row", None, None, None),
            P("seq", "row", None),
            P("seq", "row", None, None),
            P(),
        ),
        out_specs=(
            P("seq", "row", None, None),
            P("seq", "row", None, None),
            P("seq", "row", None, None),
        ),
        check_vma=False,
    )
```
